32 devices in a mesh: seg: 8 (over z, y), ctl: 4 (over x, core).
Axes of the slice: x: 2, y: 2, z: 4, core: 2. Of those that a mesh axis runs over, the one named last changes fastest.
Arguments:
- transition: float32 [8, 1024, 1024], P('seg'), may hold values from -1 to 1
- control_map: float32 [8, 1024, 256], P('seg'), may hold values from -1.5 to 1.5
- weights: float32 [8, 1024], P('seg'), may hold values from 0.01 to 0.5
Outputs:
- sensitivity: float32 [8, 1024, 2048], P('seg', None, 'ctl')
- hessian_tiles: float32 [4, 512, 512], P('ctl', 'seg')
The draws below stay inside these ranges and needn't reach their ends.
All inputs are finite; a program needn't handle non-finite values.
Results may differ from the reference program's by a relative error of at most 0.0003.
Values sent between devices are 32-bit elements; how exact they have to be, the bound alone decides.
No kernel may reach another device: no remote copies, remote signals or barrier semaphores. Data moves between devices by JAX's collectives and lax.ppermute only.
A program may use at most 128 MiB of HBM per device.

```python
import math
import jax
import jax.numpy as jnp
from jax import lax

NX = 1024
NU = 256
NSEG = 8
N_CTL = 4


def draw_transition(key, part):
    key_rate = jax.random.fold_in(key, 11)
    key_off = jax.random.fold_in(key, 12)
    log_rate = jax.random.uniform(key_rate, (NSEG, NX), jnp.float32, jnp.log(0.01), jnp.log(0.6))
    diag_vals = 1.0 - jnp.exp(log_rate)
    off_vals = jax.random.normal(key_off, (NSEG, NX, NX), jnp.float32) * (0.2 / jnp.sqrt(NX * 1.0))
    off_vals = jnp.clip(off_vals, -0.5, 0.5)
    row_ids = jax.lax.broadcasted_iota(jnp.int32, (NSEG, NX, NX), 1)
    col_ids = jax.lax.broadcasted_iota(jnp.int32, (NSEG, NX, NX), 2)
    on_diag = (row_ids == col_ids).astype(jnp.float32)
    return on_diag * diag_vals[:, :, None] + (1.0 - on_diag) * off_vals


def block_scale(own_key, dims, pieces, low, high):
    level, own = 1.0, jax.random.fold_in(own_key, 6)
    for axis_at, blocks in pieces:
        heights = jnp.exp(jax.random.uniform(jax.random.fold_in(own, axis_at), (blocks,), jnp.float32, low / len(pieces), high / len(pieces)))
        level = level * jnp.repeat(heights, dims[axis_at] // blocks).reshape([-1 if axis == axis_at else 1 for axis in range(len(dims))])
    return level


def centred(key, extent, width, most, pieces=(), kind=jnp.bfloat16):
    gain = block_scale(key, extent, pieces, -0.22, 0.18) if pieces else 1.0
    entries = jax.random.normal(key, extent, jnp.float32) * width * gain
    return jnp.minimum(jnp.maximum(entries, -most), most).astype(kind)


def setup_inputs(seed: int = 0) -> dict:
    key_of = jax.random.split(jax.random.key(seed), 4)
    transition = draw_transition(jax.random.fold_in(key_of[3], 71), 0)
    control_map = centred(key_of[1], (NSEG, NX, NU), 0.25, 1.5, ((0, 8),), jnp.float32)
    weights = jnp.clip(jnp.exp(math.log(0.5) - 3.912023 * jax.random.uniform(key_of[2], (NSEG, NX), jnp.float32) ** block_scale(key_of[2], (NSEG, NX), ((0, 8),), -0.2, 0.2)), 0.01, 0.5)
    return dict(transition=transition, control_map=control_map, weights=weights)


def reference(transition, control_map, weights):
    nseg = transition.shape[0]
    ncol = 2 * N_CTL
    stride = nseg // ncol
    col_segment = jnp.arange(ncol, dtype=jnp.int32) * stride
    group_width = 2 * NU

    def advance(carry, inputs):
        carried, hess_acc = carry
        trans_mat, input_mat, weight_row, seg_pos = inputs
        active = (col_segment == seg_pos).astype(jnp.float32)
        forcing = (active[:, None, None] * input_mat[None, :, :]).transpose(1, 0, 2).reshape(NX, ncol * NU)
        fresh = jnp.dot(trans_mat, carried, precision=lax.Precision.HIGHEST, preferred_element_type=jnp.float32) + forcing
        grouped = fresh.reshape(NX, N_CTL, group_width)
        weighted = grouped * weight_row[:, None, None]
        hess_acc = hess_acc + jnp.einsum('xca,xcb->cab', grouped, weighted, precision=lax.Precision.HIGHEST)
        return (fresh, hess_acc), fresh

    start = (jnp.zeros((NX, ncol * NU), jnp.float32), jnp.zeros((N_CTL, group_width, group_width), jnp.float32))
    (last_state, hessian_tiles), sensitivity = lax.scan(advance, start, (transition, control_map, weights, jnp.arange(nseg, dtype=jnp.int32)))
    return sensitivity, hessian_tiles
```

```python
import jax
import jax.numpy as jnp
from jax import lax
from jax.sharding import PartitionSpec as P


def dot_last(left, right):
    return lax.dot_general(
        left,
        right,
        (((1,), (1,)), ((), ())),
        precision=lax.Precision.HIGH,
        preferred_element_type=jnp.float32,
    )


def wave_pairs(nseg, tick):
    pairs = [(i, i + 1) for i in range(tick - 1, nseg - 1)] + [(nseg - 1, tick - 1)]
    idle = tick - 1
    pairs += [(i, i ^ 1 if (i ^ 1) < idle else i) for i in range(idle)]
    return pairs


def xor_swap(value, axis, by):
    devices = lax.axis_size(axis)
    return lax.ppermute(value, axis, [(i, i ^ by) for i in range(devices)])


def local(transition, control_map, weights):
    trans = transition[0]
    weight_row = weights[0]
    nseg = lax.axis_size("seg")
    nctl = lax.axis_size("ctl")
    seg = lax.axis_index("seg")
    ctl = lax.axis_index("ctl")
    core = ctl % 2
    nchip = nctl // 2
    stride = nseg // (2 * nctl)
    nu = control_map.shape[2]
    width = nu // nctl

    piece = lax.dynamic_slice_in_dim(control_map[0], ctl * width, width, 1).T
    newest = [piece]

    def sent(target_chip, slot):
        start = (4 * target_chip + slot) * stride
        age = seg - start
        known = newest[: nseg - slot * stride]
        picked = lax.select_n(jnp.clip(age, 0, len(known) - 1), *known) if len(known) > 1 else known[0]
        return jnp.where(age >= 0, picked, 0.0)

    held = {}

    def exchange(slot):
        chip = ctl // 2
        for r in range(nchip):
            out = sent(chip ^ r, slot)
            held[slot, r] = out if r == 0 else xor_swap(out, "ctl", 2 * r)

    after = {nseg - 1 - slot * stride: slot for slot in range(4)}
    for tick in range(1, nseg):
        moved = lax.ppermute(newest[-1], "seg", wave_pairs(nseg, tick))
        newest.append(dot_last(moved, trans))
        if tick in after:
            exchange(after[tick])

    blocks = []
    for half in (1, 0):
        mine = jnp.stack([jnp.where(core == 0, held[half, r], held[half + 2, r]) for r in range(nchip)])
        other = jnp.stack([jnp.where(core == 0, held[half + 2, r], held[half, r]) for r in range(nchip)])
        got = xor_swap(other, "ctl", 1)
        rows = [None] * nctl
        chip = ctl // 2
        for x in range(nchip):
            own = lax.dynamic_index_in_dim(mine, chip ^ x, 0, False)
            far = lax.dynamic_index_in_dim(got, chip ^ x, 0, False)
            rows[2 * x] = jnp.where(core == 0, own, far)
            rows[2 * x + 1] = jnp.where(core == 0, far, own)
        blocks.append(jnp.concatenate(rows, axis=0))
    sens_t = jnp.concatenate([blocks[1], blocks[0]], axis=0)

    tile = dot_last(sens_t, sens_t * weight_row[None, :])
    row_count = tile.shape[0] // nseg
    parts = lax.all_to_all(tile.reshape(nseg, row_count, -1), "seg", 0, 0, tiled=True)
    return (sens_t.T[None], parts.sum(axis=0)[None])


def solution(mesh):
    return jax.shard_map(
        local,
        mesh=mesh,
        in_specs=(P("seg", None, None), P("seg", None, None), P("seg", None)),
        out_specs=(P("seg", None, "ctl"), P("ctl", "seg", None)),
        check_vma=False,
    )
```

```python
import functools

import jax
import jax.numpy as jnp
from jax import lax
from jax.experimental import pallas as pl
from jax.experimental.pallas import tpu as pltpu
from jax.sharding import PartitionSpec as P


F32, BF16 = jnp.float32, jnp.bfloat16
VMEM = pl.BlockSpec(memory_space=pltpu.VMEM)


def size_of(shape, dtype):
    total = jnp.dtype(dtype).itemsize
    for dim in shape:
        total *= dim
    return total


def call(kernel, outs, *args, scratch=(), flops=0, extra=4 << 20):
    moved = sum(size_of(a.shape, a.dtype) for a in args) + sum(size_of(o.shape, o.dtype) for o in outs)
    used = moved + sum(size_of(m.shape, m.dtype) for m in scratch) + extra
    return pl.pallas_call(
        kernel,
        out_shape=outs,
        in_specs=[VMEM] * len(args),
        out_specs=[VMEM] * len(outs),
        scratch_shapes=scratch,
        cost_estimate=pl.CostEstimate(flops=flops, bytes_accessed=moved, transcendentals=0),
        compiler_params=pltpu.CompilerParams(vmem_limit_bytes=min(used, 60 << 20)),
    )(*args)


def out(shape, dtype=F32):
    return jax.ShapeDtypeStruct(shape, dtype)


def split(value):
    high = value.astype(BF16)
    return high, (value - high.astype(F32)).astype(BF16)


def split_kernel(trans_ref, control_ref, high_ref, low_ref, start_ref):
    rows = trans_ref.shape[0]
    for i in range(0, rows, 128):
        for k in range(0, control_ref.shape[1], 128):
            start_ref[k : k + 128, i : i + 128] = control_ref[i : i + 128, k : k + 128].T
    for i in range(0, rows, 128):
        high, low = split(trans_ref[i : i + 128, :])
        high_ref[:, i : i + 128] = high.T
        low_ref[:, i : i + 128] = low.T


def step_kernel(x_ref, high_ref, low_ref, y_ref):
    rows = x_ref.shape[0]
    high, low = split(x_ref[...])
    both = jnp.concatenate([high, low], axis=0)
    for col in range(0, y_ref.shape[1], 256):
        at = slice(col, col + 256)
        first = jnp.dot(both, high_ref[:, at], preferred_element_type=F32)
        second = jnp.dot(high, low_ref[:, at], preferred_element_type=F32)
        y_ref[:, at] = first[:rows] + (first[rows:] + second)


def gram3(left_high, left_low, right_high, right_low):
    dims = (((1,), (1,)), ((), ()))
    rows = left_high.shape[0]
    both = jnp.concatenate([left_high, left_low], axis=0)
    first = lax.dot_general(both, right_high, dims, preferred_element_type=F32)
    second = lax.dot_general(left_high, right_low, dims, preferred_element_type=F32)
    return first[:rows] + (first[rows:] + second)


class Layout:
    def __init__(self, nseg, nctl, nu, ticks):
        self.nseg, self.nctl, self.nu, self.ticks = nseg, nctl, nu, ticks
        self.stride = nseg // (2 * nctl)
        self.width = nu // nctl

    def gather(self, dst, pair, start_ref, piece_refs, limit):
        seg = lax.axis_index("seg")
        ctl = lax.axis_index("ctl")
        chip, core = ctl // 2, ctl % 2
        for b in range(2):
            age = seg - (2 * pair + b) * self.stride
            base = b * self.nu

            @pl.when((age < 0) | (age >= limit))
            def _():
                dst[base : base + self.nu, :] = jnp.zeros((self.nu, dst.shape[1]), F32)

            if start_ref is not None:

                @pl.when(age == 0)
                def _():
                    dst[base : base + self.nu, :] = start_ref[...]

            for n, tick in enumerate(self.ticks):

                @pl.when(age == tick)
                def _():
                    for r in range(self.nctl // 2):
                        for e in range(2):
                            owner = 2 * (chip ^ r) + (core ^ e)
                            at = pl.multiple_of(base + owner * self.width, self.width)
                            dst[pl.ds(at, self.width), :] = piece_refs[n * self.nctl + 2 * r + e][...]


def early_kernel(layout, weight_ref, start_ref, *refs):
    nseg, pieces = layout.nseg, len(layout.ticks) * layout.nctl
    piece_refs, out_refs = refs[:pieces], refs[pieces : pieces + nseg]
    sens, high, low, w_high, w_low, tile = refs[pieces + nseg :]
    layout.gather(sens, lax.axis_index("ctl"), start_ref, piece_refs, nseg - 2)
    for i in range(0, sens.shape[0], 128):
        at = slice(i, i + 128)
        high[at, :], low[at, :] = split(sens[at, :])
        w_high[at, :], w_low[at, :] = split(sens[at, :] * weight_ref[...])
    nu = layout.nu
    tile[:nu, :nu] = gram3(high[:nu, :], low[:nu, :], w_high[:nu, :], w_low[:nu, :])
    tile[:, nu:] = gram3(high[...], low[...], w_high[nu:, :], w_low[nu:, :])
    for i in range(0, nu, 128):
        for k in range(0, nu, 128):
            tile[nu + k : nu + k + 128, i : i + 128] = tile[i : i + 128, nu + k : nu + k + 128].T
    seg = lax.axis_index("seg")
    rows = tile.shape[0] // nseg
    for r in range(nseg):
        out_refs[r][...] = tile[pl.ds(pl.multiple_of((seg ^ r) * rows, rows), rows), :]


def late_kernel(layout, weight_ref, *refs):
    nseg, nu, width = layout.nseg, layout.nu, layout.width
    pieces = len(layout.ticks) * layout.nctl
    piece_refs, out_refs = refs[:pieces], refs[pieces:-3]
    sens, high, low = refs[-3:]
    layout.gather(sens, 0, None, piece_refs, nseg)
    seg = lax.axis_index("seg")
    own = pl.multiple_of(lax.axis_index("ctl") * width, width)
    for i in range(0, sens.shape[0], 128):
        high[i : i + 128, :], low[i : i + 128, :] = split(sens[i : i + 128, :])
    both = jnp.concatenate([sens[pl.ds(own, width), :], sens[pl.ds(own + nu, width), :]], axis=0)
    own_high, own_low = split(both * weight_ref[...])
    left = gram3(own_high, own_low, high[:nu, :], low[:nu, :])
    right = gram3(own_high, own_low, high[nu:, :], low[nu:, :])
    rows = out_refs[0].shape[0]
    last = seg == nseg - 1
    second_late = (seg - layout.stride) >= nseg - 2
    for i in range(layout.stride):
        at = slice(i * rows, (i + 1) * rows)
        to = slice(width + i * rows, width + (i + 1) * rows)
        upper = jnp.concatenate([left[at], right[at]], axis=1)
        lower = jnp.concatenate([left[to], jnp.where(second_late, right[to], 0.0)], axis=1)
        out_refs[2 * i][...] = jnp.where(last, upper, lower)
        out_refs[2 * i + 1][...] = jnp.where(last, lower, upper)


def place_kernel(layout, start_ref, *refs):
    pieces = len(layout.ticks) * layout.nctl
    piece_refs, (sens_ref, sens) = refs[:pieces], refs[pieces:]
    layout.gather(sens, lax.axis_index("ctl"), start_ref, piece_refs, layout.nseg)
    for i in range(0, sens.shape[0], 128):
        for k in range(0, sens.shape[1], 128):
            sens_ref[k : k + 128, i : i + 128] = sens[i : i + 128, k : k + 128].T


def wave_pairs(nseg, tick):
    pairs = [(i, i + 1) for i in range(tick - 1, nseg - 1)] + [(nseg - 1, tick - 1)]
    idle = tick - 1
    pairs += [(i, i ^ 1 if (i ^ 1) < idle else i) for i in range(idle)]
    return pairs


def xor_swap(value, axis, by):
    devices = lax.axis_size(axis)
    return lax.ppermute(value, axis, [(i, i ^ by) for i in range(devices)])


def local(transition, control_map, weights):
    trans = transition[0]
    nseg = lax.axis_size("seg")
    nctl = lax.axis_size("ctl")
    nx, nu = control_map.shape[1], control_map.shape[2]
    stride = nseg // (2 * nctl)
    width = nu // nctl
    rows = 2 * nu // nseg

    newest = lax.dynamic_slice_in_dim(control_map[0], lax.axis_index("ctl") * width, width, 1).T
    high, low, start = call(
        split_kernel, [out(trans.shape, BF16)] * 2 + [out((nu, nx))], trans, control_map[0]
    )

    pieces = {}
    early = None
    for tick in range(1, nseg):
        moved = lax.ppermute(newest, "seg", wave_pairs(nseg, tick))
        (newest,) = call(
            step_kernel, [out(newest.shape)], moved, high, low, flops=6 * width * nx * nx
        )
        group = []
        for r in range(nctl // 2):
            here = newest
            if r:
                here = xor_swap(newest, "ctl", 2 * r)
            there = xor_swap(here, "ctl", 1)
            group += [here, there]
        pieces[tick] = group

    def kernel_of(kernel, ticks):
        layout = Layout(nseg, nctl, nu, ticks)
        return functools.partial(kernel, layout), [p for t in ticks for p in pieces[t]]

    tall = (2 * nu, nx)
    body, given = kernel_of(early_kernel, list(range(1, nseg - 2)))
    early = call(
            body,
        [out((rows, 2 * nu))] * nseg,
        weights,
        start,
        *given,
        scratch=[pltpu.VMEM(tall, F32)] + [pltpu.VMEM(tall, BF16)] * 4 + [pltpu.VMEM((2 * nu, 2 * nu), F32)],
        flops=6 * nx * (2 * nu) ** 2,
    )
    total = early[0]
    terms = []
    for r in range(1, nseg):
        terms.append(xor_swap(early[r], "seg", r))

    late_ticks = sorted({nseg - 1 - stride, nseg - 2 - stride, nseg - 2, nseg - 1})
    body, given = kernel_of(late_kernel, late_ticks)
    late = call(
            body,
        [out((rows, 2 * nu))] * (2 * stride),
        weights,
        *given,
        scratch=[pltpu.VMEM(tall, F32)] + [pltpu.VMEM(tall, BF16)] * 2,
        flops=6 * nx * 2 * width * 2 * nu,
    )
    for i in range(stride):
        for half in range(2):
            pairs = []
            for c in range(nctl):
                near = half * (nseg // 2) + c * stride + i
                other = (1 - half) * (nseg // 2) + c * stride + i
                pairs.append(((nseg - 1) * nctl + c, near * nctl))
                pairs.append(((nseg - 2) * nctl + c, other * nctl))
            terms.append(lax.ppermute(late[2 * i + half], ("seg", "ctl"), pairs))

    body, given = kernel_of(place_kernel, list(range(1, nseg)))
    (sens,) = call(body, [out((nx, 2 * nu))], start, *given, scratch=[pltpu.VMEM(tall, F32)])
    for term in terms:
        total = total + term
    return (sens[None], total[None])


def solution(mesh):
    return jax.shard_map(
        local,
        mesh=mesh,
        in_specs=(P("seg", None, None), P("seg", None, None), P("seg", None)),
        out_specs=(P("seg", None, "ctl"), P("ctl", "seg", None)),
        check_vma=False,
    )
```

```python
import functools

import jax
import jax.numpy as jnp
from jax import lax
from jax.experimental import pallas as pl
from jax.experimental.pallas import tpu as pltpu
from jax.sharding import PartitionSpec as P


F32, BF16 = jnp.float32, jnp.bfloat16
VMEM = pl.BlockSpec(memory_space=pltpu.VMEM)


def size_of(shape, dtype):
    total = jnp.dtype(dtype).itemsize
    for dim in shape:
        total *= dim
    return total


def call(kernel, outs, *args, scratch=(), flops=0, extra=4 << 20):
    moved = sum(size_of(a.shape, a.dtype) for a in args) + sum(size_of(o.shape, o.dtype) for o in outs)
    used = moved + sum(size_of(m.shape, m.dtype) for m in scratch) + extra
    return pl.pallas_call(
        kernel,
        out_shape=outs,
        in_specs=[VMEM] * len(args),
        out_specs=[VMEM] * len(outs),
        scratch_shapes=scratch,
        cost_estimate=pl.CostEstimate(flops=flops, bytes_accessed=moved, transcendentals=0),
        compiler_params=pltpu.CompilerParams(vmem_limit_bytes=min(used, 60 << 20)),
    )(*args)


def out(shape, dtype=F32):
    return jax.ShapeDtypeStruct(shape, dtype)


def split(value):
    high = value.astype(BF16)
    return high, (value - high.astype(F32)).astype(BF16)


def split_kernel(trans_ref, control_ref, high_ref, low_ref, start_ref):
    rows = trans_ref.shape[0]
    for i in range(0, rows, 128):
        for k in range(0, control_ref.shape[1], 128):
            start_ref[k : k + 128, i : i + 128] = control_ref[i : i + 128, k : k + 128].T
    for i in range(0, rows, 128):
        high, low = split(trans_ref[i : i + 128, :])
        high_ref[:, i : i + 128] = high.T
        low_ref[:, i : i + 128] = low.T


def step_kernel(x_ref, high_ref, low_ref, y_ref):
    rows = x_ref.shape[0]
    high, low = split(x_ref[...])
    both = jnp.concatenate([high, low], axis=0)
    for col in range(0, y_ref.shape[1], 256):
        at = slice(col, col + 256)
        first = jnp.dot(both, high_ref[:, at], preferred_element_type=F32)
        second = jnp.dot(high, low_ref[:, at], preferred_element_type=F32)
        y_ref[:, at] = first[:rows] + (first[rows:] + second)


def gram3(left_high, left_low, right_high, right_low):
    dims = (((1,), (1,)), ((), ()))
    rows = left_high.shape[0]
    both = jnp.concatenate([left_high, left_low], axis=0)
    first = lax.dot_general(both, right_high, dims, preferred_element_type=F32)
    second = lax.dot_general(left_high, right_low, dims, preferred_element_type=F32)
    return first[:rows] + (first[rows:] + second)


class Layout:
    def __init__(self, nseg, nctl, nu, ticks):
        self.nseg, self.nctl, self.nu, self.ticks = nseg, nctl, nu, ticks
        self.stride = nseg // (2 * nctl)
        self.width = nu // nctl

    def gather(self, dst, pair, start_ref, piece_refs, limit):
        seg = lax.axis_index("seg")
        ctl = lax.axis_index("ctl")
        chip, core = ctl // 2, ctl % 2
        for b in range(2):
            age = seg - (2 * pair + b) * self.stride
            base = b * self.nu

            @pl.when((age < 0) | (age >= limit))
            def _():
                dst[base : base + self.nu, :] = jnp.zeros((self.nu, dst.shape[1]), F32)

            if start_ref is not None:

                @pl.when(age == 0)
                def _():
                    dst[base : base + self.nu, :] = start_ref[...]

            for n, tick in enumerate(self.ticks):

                @pl.when(age == tick)
                def _():
                    for r in range(self.nctl // 2):
                        for e in range(2):
                            owner = 2 * (chip ^ r) + (core ^ e)
                            at = pl.multiple_of(base + owner * self.width, self.width)
                            dst[pl.ds(at, self.width), :] = piece_refs[n * self.nctl + 2 * r + e][...]


def early_kernel(layout, weight_ref, start_ref, *refs):
    nseg, pieces = layout.nseg, len(layout.ticks) * layout.nctl
    piece_refs, out_refs = refs[:pieces], refs[pieces:-6]
    sens, high, low, w_high, w_low, tile = refs[-6:]
    layout.gather(sens, lax.axis_index("ctl"), start_ref, piece_refs, nseg - 2)
    for i in range(0, sens.shape[0], 128):
        at = slice(i, i + 128)
        high[at, :], low[at, :] = split(sens[at, :])
        w_high[at, :], w_low[at, :] = split(sens[at, :] * weight_ref[...])
    nu = layout.nu
    tile[:nu, :nu] = gram3(high[:nu, :], low[:nu, :], w_high[:nu, :], w_low[:nu, :])
    tile[:, nu:] = gram3(high[...], low[...], w_high[nu:, :], w_low[nu:, :])
    for i in range(0, nu, 128):
        for k in range(0, nu, 128):
            tile[nu + k : nu + k + 128, i : i + 128] = tile[i : i + 128, nu + k : nu + k + 128].T
    seg = lax.axis_index("seg")
    rows = tile.shape[0] // nseg
    for r, out_ref in enumerate(out_refs):
        out_ref[...] = tile[pl.ds(pl.multiple_of((seg ^ r) * rows, rows), rows), :]


def merge_kernel(*refs):
    *term_refs, sum_ref = refs
    sum_ref[...] = sum(ref[...] for ref in term_refs)


def late_kernel(layout, weight_ref, *refs):
    nseg, nu, width = layout.nseg, layout.nu, layout.width
    pieces = len(layout.ticks) * layout.nctl
    piece_refs, out_refs = refs[:pieces], refs[pieces:-3]
    sens, high, low = refs[-3:]
    layout.gather(sens, 0, None, piece_refs, nseg)
    seg = lax.axis_index("seg")
    own = pl.multiple_of(lax.axis_index("ctl") * width, width)
    for i in range(0, sens.shape[0], 128):
        high[i : i + 128, :], low[i : i + 128, :] = split(sens[i : i + 128, :])
    both = jnp.concatenate([sens[pl.ds(own, width), :], sens[pl.ds(own + nu, width), :]], axis=0)
    own_high, own_low = split(both * weight_ref[...])
    left = gram3(own_high, own_low, high[:nu, :], low[:nu, :])
    right = gram3(own_high, own_low, high[nu:, :], low[nu:, :])
    rows = out_refs[0].shape[0]
    last = seg == nseg - 1
    second_late = (seg - layout.stride) >= nseg - 2
    for i in range(layout.stride):
        at = slice(i * rows, (i + 1) * rows)
        to = slice(width + i * rows, width + (i + 1) * rows)
        upper = jnp.concatenate([left[at], right[at]], axis=1)
        lower = jnp.concatenate([left[to], jnp.where(second_late, right[to], 0.0)], axis=1)
        out_refs[2 * i][...] = jnp.where(last, upper, lower)
        out_refs[2 * i + 1][...] = jnp.where(last, lower, upper)


def place_kernel(layout, start_ref, *refs):
    pieces = len(layout.ticks) * layout.nctl
    piece_refs, (sens_ref, sens) = refs[:pieces], refs[pieces:]
    layout.gather(sens, lax.axis_index("ctl"), start_ref, piece_refs, layout.nseg)
    for i in range(0, sens.shape[0], 128):
        for k in range(0, sens.shape[1], 128):
            sens_ref[k : k + 128, i : i + 128] = sens[i : i + 128, k : k + 128].T


def wave_pairs(nseg, tick):
    pairs = [(i, i + 1) for i in range(tick - 1, nseg - 1)] + [(nseg - 1, tick - 1)]
    idle = tick - 1
    pairs += [(i, i ^ 1 if (i ^ 1) < idle else i) for i in range(idle)]
    return pairs


def xor_swap(value, axis, by):
    devices = lax.axis_size(axis)
    return lax.ppermute(value, axis, [(i, i ^ by) for i in range(devices)])


def local(transition, control_map, weights):
    trans = transition[0]
    nseg = lax.axis_size("seg")
    nctl = lax.axis_size("ctl")
    nx, nu = control_map.shape[1], control_map.shape[2]
    stride = nseg // (2 * nctl)
    width = nu // nctl
    rows = 2 * nu // nseg

    newest = lax.dynamic_slice_in_dim(control_map[0], lax.axis_index("ctl") * width, width, 1).T
    high, low, start = call(
        split_kernel, [out(trans.shape, BF16)] * 2 + [out((nu, nx))], trans, control_map[0]
    )

    pieces = {}
    early = None
    for tick in range(1, nseg):
        moved = lax.ppermute(newest, "seg", wave_pairs(nseg, tick))
        (newest,) = call(
            step_kernel, [out(newest.shape)], moved, high, low, flops=6 * width * nx * nx
        )
        group = []
        for r in range(nctl // 2):
            here = newest
            if r:
                here = xor_swap(newest, "ctl", 2 * r)
            there = xor_swap(here, "ctl", 1)
            group += [here, there]
        pieces[tick] = group

    def kernel_of(kernel, ticks):
        layout = Layout(nseg, nctl, nu, ticks)
        return functools.partial(kernel, layout), [p for t in ticks for p in pieces[t]]

    tall = (2 * nu, nx)
    body, given = kernel_of(early_kernel, list(range(1, nseg - 2)))
    early = call(
        body,
        [out((rows, 2 * nu))] * nseg,
        weights,
        start,
        *given,
        scratch=[pltpu.VMEM(tall, F32)]
        + [pltpu.VMEM(tall, BF16)] * 4
        + [pltpu.VMEM((2 * nu, 2 * nu), F32)],
        flops=6 * nx * (2 * nu) ** 2,
    )
    half = nseg // 2
    terms = {}
    for r in range(1, half):
        for base in (half, 0):
            terms[base + r] = xor_swap(early[base + r], "seg", r)
    (far,) = call(
        merge_kernel, [out((rows, 2 * nu))], early[half], *[terms[half + r] for r in range(1, half)]
    )
    far = xor_swap(far, "seg", half)
    total = early[0]
    terms = [terms[r] for r in range(1, half)] + [far]

    late_ticks = sorted({nseg - 1 - stride, nseg - 2 - stride, nseg - 2, nseg - 1})
    body, given = kernel_of(late_kernel, late_ticks)
    late = call(
        body,
        [out((rows, 2 * nu))] * (2 * stride),
        weights,
        *given,
        scratch=[pltpu.VMEM(tall, F32)] + [pltpu.VMEM(tall, BF16)] * 2,
        flops=6 * nx * 2 * width * 2 * nu,
    )
    for i in range(stride):
        for half in range(2):
            pairs = []
            for c in range(nctl):
                near = half * (nseg // 2) + c * stride + i
                other = (1 - half) * (nseg // 2) + c * stride + i
                pairs.append(((nseg - 1) * nctl + c, near * nctl))
                pairs.append(((nseg - 2) * nctl + c, other * nctl))
            terms.append(lax.ppermute(late[2 * i + half], ("seg", "ctl"), pairs))

    body, given = kernel_of(place_kernel, list(range(1, nseg)))
    (sens,) = call(body, [out((nx, 2 * nu))], start, *given, scratch=[pltpu.VMEM(tall, F32)])
    for term in terms:
        total = total + term
    return (sens[None], total[None])


def solution(mesh):
    return jax.shard_map(
        local,
        mesh=mesh,
        in_specs=(P("seg", None, None), P("seg", None, None), P("seg", None)),
        out_specs=(P("seg", None, "ctl"), P("ctl", "seg", None)),
        check_vma=False,
    )
```

```python
import functools

import jax
import jax.numpy as jnp
from jax import lax
from jax.experimental import pallas as pl
from jax.experimental.pallas import tpu as pltpu
from jax.sharding import PartitionSpec as P


F32, BF16 = jnp.float32, jnp.bfloat16
VMEM = pl.BlockSpec(memory_space=pltpu.VMEM)


def size_of(shape, dtype):
    total = jnp.dtype(dtype).itemsize
    for dim in shape:
        total *= dim
    return total


def call(kernel, outs, *args, scratch=(), flops=0, extra=4 << 20):
    moved = sum(size_of(a.shape, a.dtype) for a in args) + sum(size_of(o.shape, o.dtype) for o in outs)
    used = moved + sum(size_of(m.shape, m.dtype) for m in scratch) + extra
    return pl.pallas_call(
        kernel,
        out_shape=outs,
        in_specs=[VMEM] * len(args),
        out_specs=[VMEM] * len(outs),
        scratch_shapes=scratch,
        cost_estimate=pl.CostEstimate(flops=flops, bytes_accessed=moved, transcendentals=0),
        compiler_params=pltpu.CompilerParams(vmem_limit_bytes=min(used, 60 << 20)),
    )(*args)


def out(shape, dtype=F32):
    return jax.ShapeDtypeStruct(shape, dtype)


def split(value):
    high = value.astype(BF16)
    return high, (value - high.astype(F32)).astype(BF16)


def split_kernel(trans_ref, control_ref, high_ref, low_ref, start_ref):
    rows = trans_ref.shape[0]
    for i in range(0, rows, 128):
        for k in range(0, control_ref.shape[1], 128):
            start_ref[k : k + 128, i : i + 128] = control_ref[i : i + 128, k : k + 128].T
    for i in range(0, rows, 128):
        high, low = split(trans_ref[i : i + 128, :])
        high_ref[:, i : i + 128] = high.T
        low_ref[:, i : i + 128] = low.T


def step_kernel(tick, x_ref, high_ref, low_ref, y_ref):
    @pl.when(lax.axis_index("seg") >= tick)
    def _():
        rows = x_ref.shape[0]
        high, low = split(x_ref[...])
        both = jnp.concatenate([high, low], axis=0)
        for col in range(0, y_ref.shape[1], 256):
            at = slice(col, col + 256)
            first = jnp.dot(both, high_ref[:, at], preferred_element_type=F32)
            second = jnp.dot(high, low_ref[:, at], preferred_element_type=F32)
            y_ref[:, at] = first[:rows] + (first[rows:] + second)


def gram3(left_high, left_low, right_high, right_low):
    dims = (((1,), (1,)), ((), ()))
    rows = left_high.shape[0]
    both = jnp.concatenate([left_high, left_low], axis=0)
    first = lax.dot_general(both, right_high, dims, preferred_element_type=F32)
    second = lax.dot_general(left_high, right_low, dims, preferred_element_type=F32)
    return first[:rows] + (first[rows:] + second)


class Layout:
    def __init__(self, nseg, nctl, nu, ticks):
        self.nseg, self.nctl, self.nu, self.ticks = nseg, nctl, nu, ticks
        self.stride = nseg // (2 * nctl)
        self.width = nu // nctl

    def gather(self, dst, pair, start_ref, piece_refs, limit):
        seg = lax.axis_index("seg")
        ctl = lax.axis_index("ctl")
        chip, core = ctl // 2, ctl % 2
        for b in range(2):
            age = seg - (2 * pair + b) * self.stride
            base = b * self.nu

            @pl.when((age < 0) | (age >= limit))
            def _():
                dst[base : base + self.nu, :] = jnp.zeros((self.nu, dst.shape[1]), F32)

            if start_ref is not None:

                @pl.when(age == 0)
                def _():
                    dst[base : base + self.nu, :] = start_ref[...]

            for n, tick in enumerate(self.ticks):

                @pl.when(age == tick)
                def _():
                    for r in range(self.nctl // 2):
                        for e in range(2):
                            owner = 2 * (chip ^ r) + (core ^ e)
                            at = pl.multiple_of(base + owner * self.width, self.width)
                            dst[pl.ds(at, self.width), :] = piece_refs[n * self.nctl + 2 * r + e][...]


def early_kernel(layout, weight_ref, start_ref, *refs):
    nseg, pieces = layout.nseg, len(layout.ticks) * layout.nctl
    piece_refs, out_refs = refs[:pieces], refs[pieces:-6]
    sens, high, low, w_high, w_low, tile = refs[-6:]
    layout.gather(sens, lax.axis_index("ctl"), start_ref, piece_refs, nseg - 2)
    for i in range(0, sens.shape[0], 128):
        at = slice(i, i + 128)
        high[at, :], low[at, :] = split(sens[at, :])
        w_high[at, :], w_low[at, :] = split(sens[at, :] * weight_ref[...])
    nu = layout.nu
    tile[:nu, :nu] = gram3(high[:nu, :], low[:nu, :], w_high[:nu, :], w_low[:nu, :])
    tile[:, nu:] = gram3(high[...], low[...], w_high[nu:, :], w_low[nu:, :])
    for i in range(0, nu, 128):
        for k in range(0, nu, 128):
            tile[nu + k : nu + k + 128, i : i + 128] = tile[i : i + 128, nu + k : nu + k + 128].T
    seg = lax.axis_index("seg")
    rows = tile.shape[0] // nseg
    for r, out_ref in enumerate(out_refs):
        out_ref[...] = tile[pl.ds(pl.multiple_of((seg ^ r) * rows, rows), rows), :]


def merge_kernel(*refs):
    *term_refs, sum_ref = refs
    sum_ref[...] = sum(ref[...] for ref in term_refs)


def late_kernel(layout, weight_ref, *refs):
    nseg, nu, width = layout.nseg, layout.nu, layout.width
    pieces = len(layout.ticks) * layout.nctl
    piece_refs, out_refs = refs[:pieces], refs[pieces:-3]
    sens, high, low = refs[-3:]

    @pl.when(lax.axis_index("seg") >= nseg - 2)
    def _():
        layout.gather(sens, 0, None, piece_refs, nseg)
        seg = lax.axis_index("seg")
        own = pl.multiple_of(lax.axis_index("ctl") * width, width)
        for i in range(0, sens.shape[0], 128):
            high[i : i + 128, :], low[i : i + 128, :] = split(sens[i : i + 128, :])
        both = jnp.concatenate([sens[pl.ds(own, width), :], sens[pl.ds(own + nu, width), :]], axis=0)
        own_high, own_low = split(both * weight_ref[...])
        left = gram3(own_high, own_low, high[:nu, :], low[:nu, :])
        right = gram3(own_high, own_low, high[nu:, :], low[nu:, :])
        rows = out_refs[0].shape[0]
        last = seg == nseg - 1
        second_late = (seg - layout.stride) >= nseg - 2
        for i in range(layout.stride):
            at = slice(i * rows, (i + 1) * rows)
            to = slice(width + i * rows, width + (i + 1) * rows)
            upper = jnp.concatenate([left[at], right[at]], axis=1)
            lower = jnp.concatenate([left[to], jnp.where(second_late, right[to], 0.0)], axis=1)
            out_refs[2 * i][...] = jnp.where(last, upper, lower)
            out_refs[2 * i + 1][...] = jnp.where(last, lower, upper)


def finish_kernel(early_terms, *refs):
    *term_refs, sum_ref = refs
    total = sum(ref[...] for ref in term_refs[:early_terms])
    sum_ref[...] = total

    @pl.when(lax.axis_index("ctl") == 0)
    def _():
        sum_ref[...] = total + sum(ref[...] for ref in term_refs[early_terms:])


def place_kernel(layout, start_ref, *refs):
    pieces = len(layout.ticks) * layout.nctl
    piece_refs, (sens_ref, sens) = refs[:pieces], refs[pieces:]
    layout.gather(sens, lax.axis_index("ctl"), start_ref, piece_refs, layout.nseg)
    for i in range(0, sens.shape[0], 128):
        for k in range(0, sens.shape[1], 128):
            sens_ref[k : k + 128, i : i + 128] = sens[i : i + 128, k : k + 128].T


def wave_pairs(nseg, nctl, tick):
    pairs = []
    for c in range(nctl):
        ring = [(s * nctl + c, (s + 1) * nctl + c) for s in range(tick - 1, nseg - 1)]
        pairs += ring + [((nseg - 1) * nctl + c, (tick - 1) * nctl + c)]
        pairs += [(s * nctl + c, s * nctl + (c ^ 1)) for s in range(tick - 1)]
    return pairs


def xor_swap(value, axis, by):
    devices = lax.axis_size(axis)
    return lax.ppermute(value, axis, [(i, i ^ by) for i in range(devices)])


def local(transition, control_map, weights):
    trans = transition[0]
    nseg = lax.axis_size("seg")
    nctl = lax.axis_size("ctl")
    nx, nu = control_map.shape[1], control_map.shape[2]
    stride = nseg // (2 * nctl)
    width = nu // nctl
    rows = 2 * nu // nseg

    newest = lax.dynamic_slice_in_dim(control_map[0], lax.axis_index("ctl") * width, width, 1).T
    high, low, start = call(
        split_kernel, [out(trans.shape, BF16)] * 2 + [out((nu, nx))], trans, control_map[0]
    )

    pieces = {}
    early = None
    for tick in range(1, nseg):
        moved = lax.ppermute(newest, ("seg", "ctl"), wave_pairs(nseg, nctl, tick))
        (newest,) = call(
            functools.partial(step_kernel, tick),
            [out(newest.shape)],
            moved,
            high,
            low,
            flops=6 * width * nx * nx,
        )
        group = []
        for r in range(nctl // 2):
            here = newest
            if r:
                here = xor_swap(newest, "ctl", 2 * r)
            there = xor_swap(here, "ctl", 1)
            group += [here, there]
        pieces[tick] = group

    def kernel_of(kernel, ticks):
        layout = Layout(nseg, nctl, nu, ticks)
        return functools.partial(kernel, layout), [p for t in ticks for p in pieces[t]]

    tall = (2 * nu, nx)
    body, given = kernel_of(early_kernel, list(range(1, nseg - 2)))
    early = call(
        body,
        [out((rows, 2 * nu))] * nseg,
        weights,
        start,
        *given,
        scratch=[pltpu.VMEM(tall, F32)]
        + [pltpu.VMEM(tall, BF16)] * 4
        + [pltpu.VMEM((2 * nu, 2 * nu), F32)],
        flops=6 * nx * (2 * nu) ** 2,
    )
    half = nseg // 2
    terms = {}
    for r in range(1, half):
        for base in (half, 0):
            terms[base + r] = xor_swap(early[base + r], "seg", r)
    (far,) = call(
        merge_kernel, [out((rows, 2 * nu))], early[half], *[terms[half + r] for r in range(1, half)]
    )
    far = xor_swap(far, "seg", half)
    terms = [early[0]] + [terms[r] for r in range(1, half)] + [far]

    late_ticks = sorted({nseg - 1 - stride, nseg - 2 - stride, nseg - 2, nseg - 1})
    body, given = kernel_of(late_kernel, late_ticks)
    late = call(
        body,
        [out((rows, 2 * nu))] * (2 * stride),
        weights,
        *given,
        scratch=[pltpu.VMEM(tall, F32)] + [pltpu.VMEM(tall, BF16)] * 2,
        flops=6 * nx * 2 * width * 2 * nu,
    )
    last = []
    for i in range(stride):
        for part in range(2):
            pairs = []
            for c in range(nctl):
                near = part * half + c * stride + i
                other = (1 - part) * half + c * stride + i
                pairs.append(((nseg - 1) * nctl + c, near * nctl))
                pairs.append(((nseg - 2) * nctl + c, other * nctl))
            last.append(lax.ppermute(late[2 * i + part], ("seg", "ctl"), pairs))

    body, given = kernel_of(place_kernel, list(range(1, nseg)))
    (sens,) = call(body, [out((nx, 2 * nu))], start, *given, scratch=[pltpu.VMEM(tall, F32)])
    (total,) = call(
        functools.partial(finish_kernel, len(terms)), [out((rows, 2 * nu))], *terms, *last
    )
    return (sens[None], total[None])


def solution(mesh):
    return jax.shard_map(
        local,
        mesh=mesh,
        in_specs=(P("seg", None, None), P("seg", None, None), P("seg", None)),
        out_specs=(P("seg", None, "ctl"), P("ctl", "seg", None)),
        check_vma=False,
    )
```

```python
import functools

import jax
import jax.numpy as jnp
from jax import lax
from jax.experimental import pallas as pl
from jax.experimental.pallas import tpu as pltpu
from jax.sharding import PartitionSpec as P


F32, BF16 = jnp.float32, jnp.bfloat16
VMEM = pl.BlockSpec(memory_space=pltpu.VMEM)


def size_of(shape, dtype):
    total = jnp.dtype(dtype).itemsize
    for dim in shape:
        total *= dim
    return total


def call(kernel, outs, *args, scratch=(), flops=0, extra=4 << 20):
    moved = sum(size_of(a.shape, a.dtype) for a in args) + sum(size_of(o.shape, o.dtype) for o in outs)
    used = moved + sum(size_of(m.shape, m.dtype) for m in scratch) + extra
    return pl.pallas_call(
        kernel,
        out_shape=outs,
        in_specs=[VMEM] * len(args),
        out_specs=[VMEM] * len(outs),
        scratch_shapes=scratch,
        cost_estimate=pl.CostEstimate(flops=flops, bytes_accessed=moved, transcendentals=0),
        compiler_params=pltpu.CompilerParams(vmem_limit_bytes=min(used, 60 << 20)),
    )(*args)


def out(shape, dtype=F32):
    return jax.ShapeDtypeStruct(shape, dtype)


def split(value):
    high = value.astype(BF16)
    return high, (value - high.astype(F32)).astype(BF16)


def split_kernel(trans_ref, control_ref, high_ref, low_ref, start_ref):
    rows = trans_ref.shape[0]
    for i in range(0, rows, 128):
        for k in range(0, control_ref.shape[1], 128):
            start_ref[k : k + 128, i : i + 128] = control_ref[i : i + 128, k : k + 128].T
    for i in range(0, rows, 128):
        high, low = split(trans_ref[i : i + 128, :])
        high_ref[:, i : i + 128] = high.T
        low_ref[:, i : i + 128] = low.T


def product(x, high_ref, low_ref, store):
    rows = x.shape[0]
    high, low = split(x)
    both = jnp.concatenate([high, low], axis=0)
    for col in range(0, high_ref.shape[1], 256):
        at = slice(col, col + 256)
        first = jnp.dot(both, high_ref[:, at], preferred_element_type=F32)
        second = jnp.dot(high, low_ref[:, at], preferred_element_type=F32)
        store(at, first[:rows] + (first[rows:] + second))


def step_kernel(tick, part, x_ref, high_ref, low_ref, *refs):
    @pl.when(lax.axis_index("seg") >= tick)
    def _():
        rows = x_ref.shape[0]

        def store(at, y):
            if part == "whole":
                whole_ref, first_ref, second_ref = refs
                whole_ref[:, at] = y
                first_ref[:, at] = y[: rows // 2]
                second_ref[:, at] = y[rows // 2 :]
            elif part == "first":
                refs[0][:, at] = y
            else:
                first_ref, whole_ref, second_ref = refs
                whole_ref[:rows, at] = first_ref[:, at]
                whole_ref[rows:, at] = y
                second_ref[:, at] = y

        product(x_ref[...], high_ref, low_ref, store)


def gram3(left_high, left_low, right_high, right_low):
    dims = (((1,), (1,)), ((), ()))
    rows = left_high.shape[0]
    both = jnp.concatenate([left_high, left_low], axis=0)
    first = lax.dot_general(both, right_high, dims, preferred_element_type=F32)
    second = lax.dot_general(left_high, right_low, dims, preferred_element_type=F32)
    return first[:rows] + (first[rows:] + second)


class Layout:
    def __init__(self, nseg, nctl, nu, ticks):
        self.nseg, self.nctl, self.nu, self.ticks = nseg, nctl, nu, ticks
        self.stride = nseg // (2 * nctl)
        self.width = nu // nctl

    def gather(self, dst, pair, start_ref, piece_refs, limit):
        seg = lax.axis_index("seg")
        ctl = lax.axis_index("ctl")
        chip, core = ctl // 2, ctl % 2
        for b in range(2):
            age = seg - (2 * pair + b) * self.stride
            base = b * self.nu

            @pl.when((age < 0) | (age >= limit))
            def _():
                dst[base : base + self.nu, :] = jnp.zeros((self.nu, dst.shape[1]), F32)

            if start_ref is not None:

                @pl.when(age == 0)
                def _():
                    dst[base : base + self.nu, :] = start_ref[...]

            for n, tick in enumerate(self.ticks):

                @pl.when(age == tick)
                def _():
                    for r in range(self.nctl // 2):
                        for e in range(2):
                            owner = 2 * (chip ^ r) + (core ^ e)
                            at = pl.multiple_of(base + owner * self.width, self.width)
                            dst[pl.ds(at, self.width), :] = piece_refs[n * self.nctl + 2 * r + e][...]


def early_kernel(layout, weight_ref, start_ref, *refs):
    nseg, pieces = layout.nseg, len(layout.ticks) * layout.nctl
    piece_refs, out_refs = refs[:pieces], refs[pieces:-6]
    sens, high, low, w_high, w_low, tile = refs[-6:]
    layout.gather(sens, lax.axis_index("ctl"), start_ref, piece_refs, nseg - 2)
    for i in range(0, sens.shape[0], 128):
        at = slice(i, i + 128)
        high[at, :], low[at, :] = split(sens[at, :])
        w_high[at, :], w_low[at, :] = split(sens[at, :] * weight_ref[...])
    nu = layout.nu
    tile[:nu, :nu] = gram3(high[:nu, :], low[:nu, :], w_high[:nu, :], w_low[:nu, :])
    tile[:, nu:] = gram3(high[...], low[...], w_high[nu:, :], w_low[nu:, :])
    for i in range(0, nu, 128):
        for k in range(0, nu, 128):
            tile[nu + k : nu + k + 128, i : i + 128] = tile[i : i + 128, nu + k : nu + k + 128].T
    seg = lax.axis_index("seg")
    rows = tile.shape[0] // nseg
    for r, out_ref in enumerate(out_refs):
        out_ref[...] = tile[pl.ds(pl.multiple_of((seg ^ r) * rows, rows), rows), :]


def merge_kernel(*refs):
    *term_refs, sum_ref = refs
    sum_ref[...] = sum(ref[...] for ref in term_refs)


def late_kernel(layout, weight_ref, *refs):
    nseg, nu, width = layout.nseg, layout.nu, layout.width
    pieces = len(layout.ticks) * layout.nctl
    piece_refs, out_refs = refs[:pieces], refs[pieces:-3]
    sens, high, low = refs[-3:]

    @pl.when(lax.axis_index("seg") >= nseg - 2)
    def _():
        layout.gather(sens, 0, None, piece_refs, nseg)
        seg = lax.axis_index("seg")
        own = pl.multiple_of(lax.axis_index("ctl") * width, width)
        for i in range(0, sens.shape[0], 128):
            high[i : i + 128, :], low[i : i + 128, :] = split(sens[i : i + 128, :])
        both = jnp.concatenate([sens[pl.ds(own, width), :], sens[pl.ds(own + nu, width), :]], axis=0)
        own_high, own_low = split(both * weight_ref[...])
        left = gram3(own_high, own_low, high[:nu, :], low[:nu, :])
        right = gram3(own_high, own_low, high[nu:, :], low[nu:, :])
        rows = out_refs[0].shape[0]
        last = seg == nseg - 1
        second_late = (seg - layout.stride) >= nseg - 2
        for i in range(layout.stride):
            at = slice(i * rows, (i + 1) * rows)
            to = slice(width + i * rows, width + (i + 1) * rows)
            upper = jnp.concatenate([left[at], right[at]], axis=1)
            lower = jnp.concatenate([left[to], jnp.where(second_late, right[to], 0.0)], axis=1)
            out_refs[2 * i][...] = jnp.where(last, upper, lower)
            out_refs[2 * i + 1][...] = jnp.where(last, lower, upper)


def finish_kernel(early_terms, *refs):
    *term_refs, sum_ref = refs
    total = sum(ref[...] for ref in term_refs[:early_terms])
    sum_ref[...] = total

    @pl.when(lax.axis_index("ctl") == 0)
    def _():
        sum_ref[...] = total + sum(ref[...] for ref in term_refs[early_terms:])


def place_kernel(layout, start_ref, *refs):
    pieces = len(layout.ticks) * layout.nctl
    piece_refs, (sens_ref, sens) = refs[:pieces], refs[pieces:]
    layout.gather(sens, lax.axis_index("ctl"), start_ref, piece_refs, layout.nseg)
    for i in range(0, sens.shape[0], 128):
        for k in range(0, sens.shape[1], 128):
            sens_ref[k : k + 128, i : i + 128] = sens[i : i + 128, k : k + 128].T


def wave_pairs(nseg, nctl, tick):
    pairs = []
    for c in range(nctl):
        ring = [(s * nctl + c, (s + 1) * nctl + c) for s in range(tick - 1, nseg - 1)]
        pairs += ring + [((nseg - 1) * nctl + c, (tick - 1) * nctl + c)]
        pairs += [(s * nctl + c, s * nctl + (c ^ 1)) for s in range(tick - 1)]
    return pairs


def xor_swap(value, axis, by):
    devices = lax.axis_size(axis)
    return lax.ppermute(value, axis, [(i, i ^ by) for i in range(devices)])


def local(transition, control_map, weights):
    trans = transition[0]
    nseg = lax.axis_size("seg")
    nctl = lax.axis_size("ctl")
    nx, nu = control_map.shape[1], control_map.shape[2]
    stride = nseg // (2 * nctl)
    width = nu // nctl
    rows = 2 * nu // nseg

    newest = lax.dynamic_slice_in_dim(control_map[0], lax.axis_index("ctl") * width, width, 1).T
    high, low, start = call(
        split_kernel, [out(trans.shape, BF16)] * 2 + [out((nu, nx))], trans, control_map[0]
    )

    pieces = {}
    early = None
    for tick in range(1, nseg):
        def wave(value):
            return lax.ppermute(value, ("seg", "ctl"), wave_pairs(nseg, nctl, tick))

        def step(part, outs, *args):
            body = functools.partial(step_kernel, tick, part)
            flops = 6 * args[0].shape[0] * nx * nx
            return call(body, [out(shape) for shape in outs], *args, flops=flops)

        part_shape = (width // 2, nx)
        if tick == 1:
            moved = wave(newest)
            newest, upper, lower = step(
                "whole", [newest.shape, part_shape, part_shape], moved, high, low
            )
        else:
            moved = [wave(upper), wave(lower)]
            (upper,) = step("first", [part_shape], moved[0], high, low)
            newest, lower = step("second", [newest.shape, part_shape], moved[1], high, low, upper)
        group = []
        for r in range(nctl // 2):
            here = newest
            if r:
                here = xor_swap(newest, "ctl", 2 * r)
            there = xor_swap(here, "ctl", 1)
            group += [here, there]
        pieces[tick] = group

    def kernel_of(kernel, ticks):
        layout = Layout(nseg, nctl, nu, ticks)
        return functools.partial(kernel, layout), [p for t in ticks for p in pieces[t]]

    tall = (2 * nu, nx)
    body, given = kernel_of(early_kernel, list(range(1, nseg - 2)))
    early = call(
        body,
        [out((rows, 2 * nu))] * nseg,
        weights,
        start,
        *given,
        scratch=[pltpu.VMEM(tall, F32)]
        + [pltpu.VMEM(tall, BF16)] * 4
        + [pltpu.VMEM((2 * nu, 2 * nu), F32)],
        flops=6 * nx * (2 * nu) ** 2,
    )
    half = nseg // 2
    terms = {}
    for r in range(1, half):
        for base in (half, 0):
            terms[base + r] = xor_swap(early[base + r], "seg", r)
    (far,) = call(
        merge_kernel, [out((rows, 2 * nu))], early[half], *[terms[half + r] for r in range(1, half)]
    )
    far = xor_swap(far, "seg", half)
    terms = [early[0]] + [terms[r] for r in range(1, half)] + [far]

    late_ticks = sorted({nseg - 1 - stride, nseg - 2 - stride, nseg - 2, nseg - 1})
    body, given = kernel_of(late_kernel, late_ticks)
    late = call(
        body,
        [out((rows, 2 * nu))] * (2 * stride),
        weights,
        *given,
        scratch=[pltpu.VMEM(tall, F32)] + [pltpu.VMEM(tall, BF16)] * 2,
        flops=6 * nx * 2 * width * 2 * nu,
    )
    last = []
    for i in range(stride):
        for part in range(2):
            pairs = []
            for c in range(nctl):
                near = part * half + c * stride + i
                other = (1 - part) * half + c * stride + i
                pairs.append(((nseg - 1) * nctl + c, near * nctl))
                pairs.append(((nseg - 2) * nctl + c, other * nctl))
            last.append(lax.ppermute(late[2 * i + part], ("seg", "ctl"), pairs))

    body, given = kernel_of(place_kernel, list(range(1, nseg)))
    (sens,) = call(body, [out((nx, 2 * nu))], start, *given, scratch=[pltpu.VMEM(tall, F32)])
    (total,) = call(
        functools.partial(finish_kernel, len(terms)), [out((rows, 2 * nu))], *terms, *last
    )
    return (sens[None], total[None])


def solution(mesh):
    return jax.shard_map(
        local,
        mesh=mesh,
        in_specs=(P("seg", None, None), P("seg", None, None), P("seg", None)),
        out_specs=(P("seg", None, "ctl"), P("ctl", "seg", None)),
        check_vma=False,
    )
```
